32 devices in a mesh: groups: 2 (over x), tm: 16 (over z, y, core).
Axes of the slice: x: 2, y: 2, z: 4, core: 2. Of those that a mesh axis runs over, the one named last changes fastest.
Arguments:
- space_time: bfloat16 [32, 512, 1024], P(('groups', 'tm')), parts along dimension 0, may hold values from -16 to 16
- w_lin: bfloat16 [1024, 3072], replicated, may hold values from -0.1875 to 0.1875
- gain_lin: bfloat16 [1024], replicated, may hold values from 0.099609375 to 1.8984375
- w_query: bfloat16 [1024, 1024], replicated, may hold values from -4 to 4
- w_kv: bfloat16 [1024, 512], replicated, may hold values from -4 to 4
- frame_attention_gain: bfloat16 [1024], replicated, may hold values from 0.099609375 to 1.8984375
Outputs:
- attended: bfloat16 [32, 512, 1024], P(('groups', 'tm')), parts along dimension 0
The draws below stay inside these ranges and needn't reach their ends.
There are 2 independent parts, one for each index of `groups`. The reference program is written for one: setup_inputs(seed, part) draws one part's arguments, and reference() takes and returns one part's arrays. A program takes and returns all parts, laid end to end along the dimension named above; an argument that names none is the same for every part. Nothing has to cross between parts.
All inputs are finite; a program needn't handle non-finite values.
Results may differ from the reference program's by a relative error of at most 0.028.
The reference program's roundings to bfloat16 on the way count: a program that leaves them out, or rounds other values in their place, can miss the bound.
Values may be sent and summed in bfloat16 or wider, within the bound.
A program may use at most 64 MiB of HBM per device.

```python
import math
import jax
import jax.numpy as jnp
from jax import lax

D = 1024
HEADS = 8
HD = 128
KVH = 2
P_SIZE = 512
SB = 16
SPAN = 128
ROWS_DEV = 512
FRAMES = 16
N_TM = 16


def draw_space_time(key, part):
    subkeys = jax.random.split(jax.random.fold_in(key, 11), 1)
    standard = jax.random.normal(subkeys[0], (N_TM, ROWS_DEV, D), jnp.float32)
    return jnp.clip(standard, -6.0, 6.0).astype(jnp.bfloat16)


def paired_weights(base_key):
    subkeys = jax.random.split(jax.random.fold_in(base_key, 23), 3)
    query_scale = 2.5 / math.sqrt(D)
    query_weight = jax.random.normal(subkeys[0], (D, HEADS * HD), jnp.float32) * query_scale
    key_weight = jax.random.normal(subkeys[1], (D, KVH * HD), jnp.float32) / math.sqrt(D)
    value_weight = jax.random.normal(subkeys[2], (D, KVH * HD), jnp.float32) / math.sqrt(D)
    joined = jnp.concatenate([key_weight, value_weight], axis=1)
    return (jnp.clip(query_weight, -4.0, 4.0), jnp.clip(joined, -4.0, 4.0))


def draw_w_query(key, part):
    return paired_weights(key)[0].astype(jnp.bfloat16)


def draw_w_kv(key, part):
    return paired_weights(key)[1].astype(jnp.bfloat16)


def centred(own_key, shape, deviation, reach, kind=jnp.bfloat16):
    values = jax.random.normal(own_key, shape, jnp.float32) * deviation
    return jnp.minimum(jnp.maximum(values, -reach), reach).astype(kind)


def setup_inputs(seed: int = 0, part: int = 0) -> dict:
    key_of = jax.random.split(jax.random.key(seed), 7)
    part_keys = jax.random.split(jax.random.fold_in(key_of[6], part), 7)
    space_time = draw_space_time(jax.random.fold_in(jax.random.fold_in(key_of[6], part), 71), part)
    w_lin = centred(key_of[1], (D, 3 * D), D ** -0.5, 0.1875)
    gain_lin = jnp.clip(1.0 + 0.18 * jax.random.normal(key_of[2], (D,), jnp.float32), 0.099609375, 1.8984375).astype(jnp.bfloat16)
    w_query = draw_w_query(jax.random.fold_in(key_of[6], 71), part)
    w_kv = draw_w_kv(jax.random.fold_in(key_of[6], 71), part)
    frame_attention_gain = jnp.clip(1.0 + 0.18 * jax.random.normal(key_of[5], (D,), jnp.float32), 0.099609375, 1.8984375).astype(jnp.bfloat16)
    return dict(space_time=space_time, w_lin=w_lin, gain_lin=gain_lin, w_query=w_query, w_kv=w_kv, frame_attention_gain=frame_attention_gain)


epsilon = 1e-06

def reference(space_time, w_lin, gain_lin, w_query, w_kv, frame_attention_gain):
    time_ranges = N_TM // SB
    causal_mask = jnp.tril(jnp.ones((SPAN, SPAN), jnp.float32)) > 0
    line_gain = gain_lin.astype(jnp.float32).reshape(HEADS, HD)
    sequences = space_time.reshape(time_ranges, SB, ROWS_DEV, D).transpose(1, 0, 2, 3).reshape(SB, time_ranges * ROWS_DEV, D)

    def block_mixer(sequence):
        packed = jnp.dot(sequence, w_lin, preferred_element_type=jnp.float32).astype(jnp.bfloat16)
        span_count = sequence.shape[0] // SPAN
        query_rows = packed[:, :D].reshape(span_count, SPAN, HEADS, HD)
        key_rows = packed[:, D:2 * D].reshape(span_count, SPAN, HEADS, HD)
        value_rows = packed[:, 2 * D:].reshape(span_count, SPAN, HEADS, HD)

        def advance(carried, pieces):
            expanded_query_heads = pieces[0].astype(jnp.float32)
            expanded_key_heads = pieces[1].astype(jnp.float32)
            value_wide = pieces[2].astype(jnp.float32)
            rounded = lax.optimization_barrier(carried.astype(jnp.bfloat16)).astype(jnp.float32)
            readout = jnp.einsum('nhd,hde->nhe', expanded_query_heads, rounded)
            attention_logits = jnp.einsum('lzx,uzx->zlu', expanded_query_heads, expanded_key_heads)
            weights = lax.optimization_barrier(jnp.where(causal_mask, attention_logits, 0.0).astype(jnp.bfloat16)).astype(jnp.float32)
            local_sum = jnp.einsum('hnm,mhe->nhe', weights, value_wide)
            updated = carried + jnp.einsum('nhd,nhe->hde', expanded_key_heads, value_wide)
            return (updated, readout + local_sum)
        _, outputs = lax.scan(advance, jnp.zeros((HEADS, HD, HD), jnp.float32), (query_rows, key_rows, value_rows))
        outputs = outputs.reshape(-1, HEADS, HD)
        mean_square = lax.optimization_barrier(jnp.mean(outputs * outputs, axis=-1, keepdims=True))
        normed = outputs * lax.rsqrt(mean_square + epsilon) * line_gain
        return (sequence.astype(jnp.float32) + normed.reshape(-1, D)).astype(jnp.bfloat16)
    hidden = lax.map(block_mixer, sequences)
    frames_all = hidden.reshape(SB, FRAMES, P_SIZE // SB, D).transpose(1, 0, 2, 3).reshape(FRAMES * P_SIZE, D)
    widened = frames_all.astype(jnp.float32)
    mean_square = lax.optimization_barrier(jnp.mean(widened * widened, axis=-1, keepdims=True))
    normed = (widened * lax.rsqrt(mean_square + epsilon) * frame_attention_gain.astype(jnp.float32)).astype(jnp.bfloat16)
    group_size = HEADS // KVH
    queries = jnp.dot(normed, w_query, preferred_element_type=jnp.float32).astype(jnp.bfloat16)
    queries = queries.reshape(FRAMES, P_SIZE, KVH, group_size, HD)
    key_value_product = jnp.dot(normed, w_kv, preferred_element_type=jnp.float32).astype(jnp.bfloat16)
    key_value_product = key_value_product.reshape(FRAMES, P_SIZE, 2 * KVH * HD)
    positions = jnp.arange(2 * P_SIZE)
    scale_factor = 1.0 / math.sqrt(HD)

    def frame_attend(frame_index):
        current = lax.dynamic_index_in_dim(key_value_product, frame_index, 0, keepdims=False)
        earlier = lax.dynamic_index_in_dim(key_value_product, jnp.maximum(frame_index - 1, 0), 0, keepdims=False)
        window = jnp.concatenate([earlier, current], axis=0)
        key_rows = window[:, :KVH * HD].reshape(2 * P_SIZE, KVH, HD).astype(jnp.float32)
        value_rows = window[:, KVH * HD:].reshape(2 * P_SIZE, KVH, HD).astype(jnp.float32)
        query_rows = lax.dynamic_index_in_dim(queries, frame_index, 0, keepdims=False).astype(jnp.float32)
        attention_logits = jnp.einsum('pkgd,mkd->kgpm', query_rows, key_rows) * scale_factor
        usable_key = (positions >= P_SIZE) | (frame_index > 0)
        attention_logits = jnp.where(usable_key, attention_logits, -jnp.inf)
        largest = lax.optimization_barrier(jnp.max(attention_logits, axis=-1, keepdims=True))
        raised = jnp.exp(attention_logits - largest)
        weights = raised / lax.optimization_barrier(jnp.sum(raised, axis=-1, keepdims=True))
        weights = lax.optimization_barrier(weights.astype(jnp.bfloat16)).astype(jnp.float32)
        result = jnp.einsum('kgpm,mkd->pkgd', weights, value_rows)
        return result.astype(jnp.bfloat16).reshape(P_SIZE, D)
    return lax.map(frame_attend, jnp.arange(FRAMES, dtype=jnp.int32))
```

```python
import functools
import math

import jax
import jax.numpy as jnp
from jax import lax
from jax.experimental import pallas as pl
from jax.experimental.pallas import tpu as pltpu
from jax.sharding import PartitionSpec as P

HEADS = 8
HD = 128
KVH = 2
P_SIZE = 512
SB = 16
SPAN = 128
PAIR = 2 * HD
STAGES = HEADS // 2
TOKENS = P_SIZE // SB
QUARTERS = 4
ROWS_Q = P_SIZE // QUARTERS
CHUNKS = [(0, 2), (2, 1), (3, 1)]

epsilon = 1e-06


def shifted(block, axis, distance):
    devices = range(lax.axis_size(axis))
    route = [(i - distance, i) for i in devices if i - distance in devices]
    return lax.ppermute(block, axis, route)


def carried_state(tokens, w_lin, count):
    width = tokens.shape[1]
    rows = tokens.shape[0]
    packed = jnp.dot(tokens, w_lin[:, width:], preferred_element_type=jnp.float32).astype(jnp.bfloat16)
    keys = packed[:, :width].reshape(rows, HEADS, HD)
    values = packed[:, width:].reshape(rows, HEADS, HD)
    total = jnp.einsum("nhd,nhe->hde", keys, values, preferred_element_type=jnp.float32)
    within = lax.axis_index("tm") // SB

    def hop(_, state):
        return jnp.where(within > 0, shifted(state + total, "tm", SB), 0.0)

    return lax.fori_loop(0, count // SB - 1, hop, jnp.zeros_like(total))


def dot(a, b):
    return jnp.dot(a, b, preferred_element_type=jnp.float32)


def dot_t(a, b):
    return lax.dot_general(a, b, (((1,), (1,)), ((), ())), preferred_element_type=jnp.float32)


def t_dot(a, b):
    return lax.dot_general(a, b, (((0,), (0,)), ((), ())), preferred_element_type=jnp.float32)


def kernel(count, *refs):
    long = count > SB
    tokens_hbm, w_lin_hbm, gain_lin, w_query_hbm, w_kv_hbm, gain_frame = refs[:6]
    refs = refs[6:]
    if long:
        incoming = refs[0]
        refs = refs[1:]
    (out_s, tokens, w_buf, wq_buf, wkv_buf, gains, qkv, hid, recv, normed, kv_own, kv_prev, queries, o_run, m_run,
     l_run, in_sem, w_sem, send_sem, recv_sem, kv_send, kv_recv) = refs
    width = tokens.shape[1]
    rows = tokens.shape[0]

    me = lax.axis_index("tm")
    position = lax.rem(me, SB)
    base = me - position
    bits = [lax.rem(position // (1 << i), 2) for i in range(4)]

    def partner(j):
        return sum(lax.rem(bits[i] + ((j >> i) & 1), 2) * (1 << i) for i in range(4))

    last = me == count - 1
    barrier = pltpu.get_barrier_semaphore()

    token_copy = pltpu.make_async_copy(tokens_hbm.at[0], tokens, in_sem.at[0])
    token_copy.start()

    def w_copy(stage, c):
        start = c * width + stage * PAIR
        if not isinstance(stage, int):
            start = pl.multiple_of(start, PAIR)
        return pltpu.make_async_copy(
            w_lin_hbm.at[:, pl.ds(start, PAIR)], w_buf.at[stage, c], w_sem.at[stage, c]
        )

    for c in range(3):
        w_copy(0, c).start()
    wkv_copy = pltpu.make_async_copy(w_kv_hbm, wkv_buf, in_sem.at[1])
    wq_copy = pltpu.make_async_copy(w_query_hbm, wq_buf, in_sem.at[2])

    beside, near, across = [1, 2, 3], [4, 5, 6, 7], list(range(8, SB))
    peers = across + near + beside
    for j in peers:
        pl.semaphore_signal(barrier, inc=1, device_id={"tm": base + partner(j)})
    if long:
        @pl.when(jnp.logical_and(position == SB - 1, jnp.logical_not(last)))
        def _():
            pl.semaphore_signal(barrier, inc=1, device_id={"tm": me + 1})

        @pl.when(jnp.logical_and(position == 0, me > 0))
        def _():
            pl.semaphore_signal(barrier, inc=1, device_id={"tm": me - 1})

    line = gain_lin[...].astype(jnp.float32).reshape(1, width)
    frame = gain_frame[...].astype(jnp.float32).reshape(1, width)
    for stage in range(STAGES):
        gains[stage] = line[:, stage * PAIR:(stage + 1) * PAIR]
        gains[STAGES + stage] = frame[:, stage * PAIR:(stage + 1) * PAIR]

    causal = lax.broadcasted_iota(jnp.int32, (SPAN, SPAN), 0) >= lax.broadcasted_iota(jnp.int32, (SPAN, SPAN), 1)

    def piece(stage, j):
        other = partner(j)
        return pltpu.make_async_remote_copy(
            src_ref=hid.at[stage, pl.ds(pl.multiple_of(other * TOKENS, TOKENS), TOKENS)],
            dst_ref=recv.at[stage, pl.ds(pl.multiple_of(position * TOKENS, TOKENS), TOKENS)],
            send_sem=send_sem.at[stage, j],
            recv_sem=recv_sem.at[stage, position],
            device_id={"tm": base + other},
        )

    def arrival(stage, j):
        other = partner(j)
        return pltpu.make_async_remote_copy(
            src_ref=hid.at[stage, pl.ds(pl.multiple_of(position * TOKENS, TOKENS), TOKENS)],
            dst_ref=recv.at[stage, pl.ds(pl.multiple_of(other * TOKENS, TOKENS), TOKENS)],
            send_sem=send_sem.at[stage, j],
            recv_sem=recv_sem.at[stage, other],
            device_id={"tm": base + other},
        )

    token_copy.wait()

    def mix(stage, _):
        for c in range(3):
            w_copy(stage, c).wait()

        @pl.when(stage + 1 < STAGES)
        def _():
            for c in range(3):
                w_copy(stage + 1, c).start()

        @pl.when(stage + 1 == STAGES)
        def _():
            wkv_copy.start()
            wq_copy.start()

        for c in range(3):
            qkv[c] = dot(tokens[...], w_buf[stage, c]).astype(jnp.bfloat16)
        for half in range(2):
            columns = slice(half * HD, (half + 1) * HD)
            if long:
                state = incoming[2 * stage + half]
            else:
                state = jnp.zeros((HD, HD), jnp.float32)
            gain = gains[stage][:, columns]
            wide = pl.ds(pl.multiple_of(stage * PAIR + half * HD, HD), HD)
            for b in range(rows // SPAN):
                span = slice(b * SPAN, (b + 1) * SPAN)
                q, k, v = qkv[0, span, columns], qkv[1, span, columns], qkv[2, span, columns]
                local = jnp.where(causal, dot_t(q, k), 0.0).astype(jnp.bfloat16)
                if b == 0 and not long:
                    mixed = dot(local, v)
                else:
                    mixed = dot(
                        jnp.concatenate([q, local], axis=1),
                        jnp.concatenate([state.astype(jnp.bfloat16), v], axis=0),
                    )
                if b + 1 < rows // SPAN:
                    state = state + t_dot(k, v)
                mean = jnp.mean(mixed * mixed, axis=-1, keepdims=True)
                grown = mixed * lax.rsqrt(mean + epsilon) * gain
                hid[stage, span, columns] = (tokens[span, wide].astype(jnp.float32) + grown).astype(jnp.bfloat16)

        @pl.when(stage == 0)
        def _():
            extra = 0
            if long:
                extra = (
                    jnp.logical_and(position == SB - 1, jnp.logical_not(last)).astype(jnp.int32)
                    + jnp.logical_and(position == 0, me > 0).astype(jnp.int32)
                )
            pl.semaphore_wait(barrier, SB - 1 + extra)

        for j in near + across[:4] + beside:
            piece(stage, j).start()

        mine = pl.ds(pl.multiple_of(position * TOKENS, TOKENS), TOKENS)
        recv[stage, mine] = hid[stage, mine]
        return 0

    lax.fori_loop(0, STAGES, mix, 0)

    for j in across[4:]:
        for stage in range(STAGES):
            piece(stage, j).start()

    def kv_copy(chunk, device):
        first, blocks = CHUNKS[chunk]
        return pltpu.make_async_remote_copy(
            src_ref=kv_own.at[:, pl.ds(first, blocks)], dst_ref=kv_prev.at[:, pl.ds(first, blocks)],
            send_sem=kv_send.at[chunk], recv_sem=kv_recv.at[chunk], device_id={"tm": device},
        )

    def kv_twice(chunk):
        first, blocks = CHUNKS[chunk]
        return pltpu.make_async_copy(
            kv_own.at[:, pl.ds(first, blocks)], kv_prev.at[:, pl.ds(first, blocks)], kv_recv.at[chunk]
        )

    def place(first, blocks):
        block = sum(lax.rem(bits[i + 2] + ((first >> i) & 1), 2) * (1 << i) for i in range(2))
        block = block // blocks * blocks
        return pl.ds(pl.multiple_of(block * ROWS_Q, blocks * ROWS_Q), blocks * ROWS_Q)

    wkv_copy.wait()
    wq_copy.wait()

    def project(chunk):
        first, blocks = CHUNKS[chunk]
        count_rows = blocks * ROWS_Q
        for stage in range(STAGES):
            for j in range(4 * first, 4 * (first + blocks)):
                if j:
                    arrival(stage, j).wait_recv()
        span = place(first, blocks)
        parts = [recv[stage, span].astype(jnp.float32) for stage in range(STAGES)]
        mean = sum(jnp.sum(p * p, axis=-1, keepdims=True) for p in parts) / width
        inverse = lax.rsqrt(mean + epsilon)
        for stage in range(STAGES):
            normed[:count_rows, stage * PAIR:(stage + 1) * PAIR] = (
                parts[stage] * inverse * gains[STAGES + stage]
            ).astype(jnp.bfloat16)
        pairs = dot(normed[:count_rows], wkv_buf[...])
        for b in range(blocks):
            rows_b = slice(b * ROWS_Q, (b + 1) * ROWS_Q)
            for i in range(KVH):
                kv_own[i, first + b] = pairs[rows_b, i * HD:(i + 1) * HD].astype(jnp.bfloat16)
                values = pairs[rows_b, (KVH + i) * HD:(KVH + i + 1) * HD]
                kv_own[KVH + i, first + b] = values.T.astype(jnp.bfloat16)

        @pl.when(jnp.logical_not(last))
        def _():
            kv_copy(chunk, me + 1).start()

        @pl.when(me == 0)
        def _():
            kv_twice(chunk).start()

        for step in range(STAGES):
            q_pair = dot(normed[:count_rows], wq_buf[:, step * PAIR:(step + 1) * PAIR]).astype(jnp.bfloat16)
            for half in range(2):
                queries[2 * step + half, first * ROWS_Q:(first + blocks) * ROWS_Q] = q_pair[:, half * HD:(half + 1) * HD]

    def earlier(chunk):
        @pl.when(me == 0)
        def _():
            kv_twice(chunk).wait()

        @pl.when(me > 0)
        def _():
            kv_copy(chunk, me - 1).wait_recv()

    factor = math.log2(math.e) / math.sqrt(HD)
    sharing = HEADS // KVH

    def attend(pieces):
        def step(kv_head, _):
            for q_first, q_blocks, blocks, fresh, final in pieces:
                columns = slice(q_first * ROWS_Q, (q_first + q_blocks) * ROWS_Q)
                keys = jnp.concatenate([ref[kv_head, b] for ref, b in blocks], axis=0)
                values = jnp.concatenate([ref[KVH + kv_head, b] for ref, b in blocks], axis=1)
                for g in range(sharing):
                    head = kv_head * sharing + g
                    s = dot_t(keys, queries[head, columns])
                    m = jnp.max(s, axis=0, keepdims=True)
                    if not fresh:
                        m = jnp.maximum(m, m_run[head, :, columns])
                    p = jnp.exp2((s - m) * factor)
                    total = jnp.sum(p, axis=0, keepdims=True)
                    o = dot(values, p.astype(jnp.bfloat16))
                    if not fresh:
                        scale = jnp.exp2((m_run[head, :, columns] - m) * factor)
                        total = total + l_run[head, :, columns] * scale
                        o = o + o_run[head, :, columns] * scale
                    if final:
                        out = (o / total).T.astype(jnp.bfloat16)
                        done = 0
                        for first, chunk_blocks in CHUNKS:
                            if q_first <= first < q_first + q_blocks:
                                size = chunk_blocks * ROWS_Q
                                out_s[head, place(first, chunk_blocks)] = out[done:done + size]
                                done += size
                    else:
                        m_run[head, :, columns] = m
                        l_run[head, :, columns] = total
                        o_run[head, :, columns] = o
            return 0

        lax.fori_loop(0, KVH, step, 0)

    own = [(kv_own, b) for b in range(QUARTERS)]
    prev = [(kv_prev, b) for b in range(QUARTERS)]
    with jax.named_scope("proj0"):
        project(0)
    with jax.named_scope("att0"):
        attend([(0, 2, own[:2], True, False)])
    with jax.named_scope("proj1"):
        project(1)
    with jax.named_scope("ear0"):
        earlier(0)
    with jax.named_scope("att1"):
        attend([(0, 2, own[2:3] + prev[:2], False, False), (2, 1, own[:3] + prev[:2], True, False)])
    with jax.named_scope("ear1"):
        earlier(1)
    with jax.named_scope("att2"):
        attend([(0, 3, prev[2:3], False, False)])
    with jax.named_scope("proj2"):
        project(2)
    with jax.named_scope("att3"):
        attend([(3, 1, own + prev[:3], True, False)])
    with jax.named_scope("ear2"):
        earlier(2)
    with jax.named_scope("att4"):
        attend([(0, 3, own[3:] + prev[3:], False, True), (3, 1, prev[3:], False, True)])

    def sent(stage, _):
        for j in peers:
            piece(stage, j).wait_send()
        return 0

    lax.fori_loop(0, STAGES, sent, 0)

    @pl.when(jnp.logical_not(last))
    def _():
        for chunk in range(len(CHUNKS)):
            kv_copy(chunk, me + 1).wait_send()


def leave(out_s, out_hbm, out_sem):
    def out_copy(step):
        return pltpu.make_async_copy(out_s.at[step], out_hbm.at[0, :, pl.ds(step * HD, HD)], out_sem.at[step])

    for step in range(HEADS):
        out_copy(step).start()
    for step in range(HEADS):
        out_copy(step).wait()


def body(count, space_time, w_lin, gain_lin, w_query, w_kv, frame_attention_gain):
    rows, width = space_time.shape[1:]
    args = [space_time, w_lin, gain_lin, w_query, w_kv, frame_attention_gain]
    hbm = pl.BlockSpec(memory_space=pltpu.HBM)
    vmem = pl.BlockSpec(memory_space=pltpu.VMEM)
    specs = [hbm, hbm, vmem, hbm, hbm, vmem]
    if count > SB:
        args.append(carried_state(space_time[0], w_lin, count))
        specs.append(vmem)
    bf16, f32 = jnp.bfloat16, jnp.float32
    heads = pl.pallas_call(
        functools.partial(kernel, count),
        out_shape=pltpu.VMEM((HEADS, P_SIZE, HD), bf16),
        in_specs=specs,
        out_specs=vmem,
        scratch_shapes=[
            pltpu.VMEM((rows, width), bf16),
            pltpu.VMEM((STAGES, 3, width, PAIR), bf16),
            pltpu.VMEM(w_query.shape, bf16),
            pltpu.VMEM(w_kv.shape, bf16),
            pltpu.VMEM((2 * STAGES, 1, PAIR), f32),
            pltpu.VMEM((3, rows, PAIR), bf16),
            pltpu.VMEM((STAGES, rows, PAIR), bf16),
            pltpu.VMEM((STAGES, P_SIZE, PAIR), bf16),
            pltpu.VMEM((2 * ROWS_Q, width), bf16),
            pltpu.VMEM((2 * KVH, QUARTERS, ROWS_Q, HD), bf16),
            pltpu.VMEM((2 * KVH, QUARTERS, ROWS_Q, HD), bf16),
            pltpu.VMEM((HEADS, P_SIZE, HD), bf16),
            pltpu.VMEM((HEADS, HD, P_SIZE), f32),
            pltpu.VMEM((HEADS, 1, P_SIZE), f32),
            pltpu.VMEM((HEADS, 1, P_SIZE), f32),
            pltpu.SemaphoreType.DMA((3,)),
            pltpu.SemaphoreType.DMA((STAGES, 3)),
            pltpu.SemaphoreType.DMA((STAGES, SB)),
            pltpu.SemaphoreType.DMA((STAGES, SB)),
            pltpu.SemaphoreType.DMA((len(CHUNKS),)),
            pltpu.SemaphoreType.DMA((len(CHUNKS),)),
        ],
        compiler_params=pltpu.CompilerParams(
            collective_id=0, has_side_effects=True, vmem_limit_bytes=60 * 1024 * 1024
        ),
        name="video_layer",
    )(*args)
    return pl.pallas_call(
        leave,
        out_shape=jax.ShapeDtypeStruct(space_time.shape, bf16),
        in_specs=[vmem],
        out_specs=hbm,
        scratch_shapes=[pltpu.SemaphoreType.DMA((HEADS,))],
        compiler_params=pltpu.CompilerParams(vmem_limit_bytes=4 * 1024 * 1024),
        name="leave",
    )(heads)


def solution(mesh):
    placed = (P(("groups", "tm"), None, None), P(), P(), P(), P(), P())
    return jax.shard_map(
        functools.partial(body, mesh.shape["tm"]),
        mesh=mesh,
        in_specs=placed,
        out_specs=P(("groups", "tm"), None, None),
        check_vma=False,
    )
```

```python
import functools
import math

import jax
import jax.numpy as jnp
from jax import lax
from jax.experimental import pallas as pl
from jax.experimental.pallas import tpu as pltpu
from jax.sharding import PartitionSpec as P

HEADS = 8
HD = 128
KVH = 2
P_SIZE = 512
SB = 16
SPAN = 128
PAIR = 2 * HD
STAGES = HEADS // 2
TOKENS = P_SIZE // SB
QUARTERS = 4
ROWS_Q = P_SIZE // QUARTERS
HALF = SB // 2
CHUNKS = [(0, 2), (2, 1), (3, 1)]

epsilon = 1e-06


def shifted(block, axis, distance):
    devices = range(lax.axis_size(axis))
    route = [(i - distance, i) for i in devices if i - distance in devices]
    return lax.ppermute(block, axis, route)


def carried_state(tokens, w_lin, count):
    width = tokens.shape[1]
    rows = tokens.shape[0]
    packed = jnp.dot(tokens, w_lin[:, width:], preferred_element_type=jnp.float32).astype(jnp.bfloat16)
    keys = packed[:, :width].reshape(rows, HEADS, HD)
    values = packed[:, width:].reshape(rows, HEADS, HD)
    total = jnp.einsum("nhd,nhe->hde", keys, values, preferred_element_type=jnp.float32)
    within = lax.axis_index("tm") // SB

    def hop(_, state):
        return jnp.where(within > 0, shifted(state + total, "tm", SB), 0.0)

    return lax.fori_loop(0, count // SB - 1, hop, jnp.zeros_like(total))


def dot(a, b):
    return jnp.dot(a, b, preferred_element_type=jnp.float32)


def dot_t(a, b):
    return lax.dot_general(a, b, (((1,), (1,)), ((), ())), preferred_element_type=jnp.float32)


def t_dot(a, b):
    return lax.dot_general(a, b, (((0,), (0,)), ((), ())), preferred_element_type=jnp.float32)


def kernel(count, *refs):
    long = count > SB
    tokens_hbm, w_lin_hbm, gain_lin, w_query_hbm, w_kv_hbm, gain_frame = refs[:6]
    refs = refs[6:]
    if long:
        incoming = refs[0]
        refs = refs[1:]
    (out_s, tokens, w_buf, wq_buf, wkv_buf, gains, qkv, hid, recv, normed, kv_own, kv_prev, queries, o_run, m_run,
     l_run, extra, in_sem, w_sem, send_sem, recv_sem, kv_send, kv_recv, extra_send, extra_recv) = refs
    width = tokens.shape[1]
    rows = tokens.shape[0]

    me = lax.axis_index("tm")
    position = lax.rem(me, SB)
    base = me - position
    bits = [lax.rem(position // (1 << i), 2) for i in range(4)]

    def partner(j):
        return sum(lax.rem(bits[i] + ((j >> i) & 1), 2) * (1 << i) for i in range(4))

    last = me == count - 1
    barrier = pltpu.get_barrier_semaphore()

    token_copy = pltpu.make_async_copy(tokens_hbm.at[0], tokens, in_sem.at[0])
    token_copy.start()

    def w_copy(stage, c):
        start = c * width + stage * PAIR
        if not isinstance(stage, int):
            start = pl.multiple_of(start, PAIR)
        return pltpu.make_async_copy(
            w_lin_hbm.at[:, pl.ds(start, PAIR)], w_buf.at[stage, c], w_sem.at[stage, c]
        )

    for c in range(3):
        w_copy(0, c).start()
    wkv_copy = pltpu.make_async_copy(w_kv_hbm, wkv_buf, in_sem.at[1])
    wq_copy = pltpu.make_async_copy(w_query_hbm, wq_buf, in_sem.at[2])

    beside, near, across = [1, 2, 3], [4, 5, 6, 7], list(range(8, SB))
    peers = across + near + beside
    for j in peers:
        pl.semaphore_signal(barrier, inc=1, device_id={"tm": base + partner(j)})
    if long:
        @pl.when(jnp.logical_and(position == SB - 1, jnp.logical_not(last)))
        def _():
            pl.semaphore_signal(barrier, inc=1, device_id={"tm": me + 1})

        @pl.when(jnp.logical_and(position == 0, me > 0))
        def _():
            pl.semaphore_signal(barrier, inc=1, device_id={"tm": me - 1})

    line = gain_lin[...].astype(jnp.float32).reshape(1, width)
    frame = gain_frame[...].astype(jnp.float32).reshape(1, width)
    for stage in range(STAGES):
        gains[stage] = line[:, stage * PAIR:(stage + 1) * PAIR]
        gains[STAGES + stage] = frame[:, stage * PAIR:(stage + 1) * PAIR]

    causal = lax.broadcasted_iota(jnp.int32, (SPAN, SPAN), 0) >= lax.broadcasted_iota(jnp.int32, (SPAN, SPAN), 1)

    def piece(stage, j):
        other = partner(j)
        return pltpu.make_async_remote_copy(
            src_ref=hid.at[stage, pl.ds(pl.multiple_of(other * TOKENS, TOKENS), TOKENS)],
            dst_ref=recv.at[stage, pl.ds(pl.multiple_of(position * TOKENS, TOKENS), TOKENS)],
            send_sem=send_sem.at[stage, j],
            recv_sem=recv_sem.at[stage, position],
            device_id={"tm": base + other},
        )

    def arrival(stage, j):
        other = partner(j)
        return pltpu.make_async_remote_copy(
            src_ref=hid.at[stage, pl.ds(pl.multiple_of(position * TOKENS, TOKENS), TOKENS)],
            dst_ref=recv.at[stage, pl.ds(pl.multiple_of(other * TOKENS, TOKENS), TOKENS)],
            send_sem=send_sem.at[stage, j],
            recv_sem=recv_sem.at[stage, other],
            device_id={"tm": base + other},
        )

    def extra_piece(stage, k):
        return pltpu.make_async_remote_copy(
            src_ref=hid.at[stage, pl.ds((HALF - 1) * TOKENS, TOKENS)],
            dst_ref=extra.at[stage, pl.ds(pl.multiple_of(k * TOKENS, TOKENS), TOKENS)],
            send_sem=extra_send.at[stage],
            recv_sem=extra_recv.at[stage, k],
            device_id={"tm": base + HALF},
        )

    token_copy.wait()

    def mix(stage, _):
        for c in range(3):
            w_copy(stage, c).wait()

        @pl.when(stage + 1 < STAGES)
        def _():
            for c in range(3):
                w_copy(stage + 1, c).start()

        @pl.when(stage + 1 == STAGES)
        def _():
            wkv_copy.start()
            wq_copy.start()

        for c in range(3):
            qkv[c] = dot(tokens[...], w_buf[stage, c]).astype(jnp.bfloat16)
        states = [incoming[2 * stage + half] if long else jnp.zeros((HD, HD), jnp.float32) for half in range(2)]

        def spans(numbers):
            for b, half in [(b, half) for b in numbers for half in range(2)]:
                columns = slice(half * HD, (half + 1) * HD)
                state = states[half]
                gain = gains[stage][:, columns]
                wide = pl.ds(pl.multiple_of(stage * PAIR + half * HD, HD), HD)
                span = slice(b * SPAN, (b + 1) * SPAN)
                q, k, v = qkv[0, span, columns], qkv[1, span, columns], qkv[2, span, columns]
                local = jnp.where(causal, dot_t(q, k), 0.0).astype(jnp.bfloat16)
                if b == 0 and not long:
                    mixed = dot(local, v)
                else:
                    mixed = dot(
                        jnp.concatenate([q, local], axis=1),
                        jnp.concatenate([state.astype(jnp.bfloat16), v], axis=0),
                    )
                if b + 1 < rows // SPAN:
                    states[half] = state + t_dot(k, v)
                mean = jnp.mean(mixed * mixed, axis=-1, keepdims=True)
                grown = mixed * lax.rsqrt(mean + epsilon) * gain
                hid[stage, span, columns] = (tokens[span, wide].astype(jnp.float32) + grown).astype(jnp.bfloat16)

        def send(group):
            for j in group:
                piece(stage, j).start()

        middle = rows // SPAN // 2
        spans(range(middle))

        @pl.when(stage == 0)
        def _():
            extra = 0
            if long:
                extra = (
                    jnp.logical_and(position == SB - 1, jnp.logical_not(last)).astype(jnp.int32)
                    + jnp.logical_and(position == 0, me > 0).astype(jnp.int32)
                )
            pl.semaphore_wait(barrier, SB - 1 + extra)

        @pl.when(jnp.logical_and(bits[3] == 1, stage < STAGES - 1))
        def _():
            send(across[:4])

        @pl.when(position > HALF)
        def _():
            extra_piece(stage, lax.rem(position, HALF)).start()

        @pl.when(position == HALF)
        def _():
            extra[stage, :TOKENS] = hid[stage, (HALF - 1) * TOKENS:HALF * TOKENS]

        @pl.when(bits[3] == 0)
        def _():
            send(near + beside)

        spans(range(middle, rows // SPAN))

        @pl.when(bits[3] == 1)
        def _():
            send(near + beside)

        @pl.when(jnp.logical_or(bits[3] == 0, stage == STAGES - 1))
        def _():
            send(across[:4])

        mine = pl.ds(pl.multiple_of(position * TOKENS, TOKENS), TOKENS)
        recv[stage, mine] = hid[stage, mine]
        return 0

    lax.fori_loop(0, STAGES, mix, 0)

    def whole(j, here, there):
        return pltpu.make_async_remote_copy(
            src_ref=hid.at[:, pl.ds(pl.multiple_of(there * TOKENS, TOKENS), TOKENS)],
            dst_ref=recv.at[:, pl.ds(pl.multiple_of(here * TOKENS, TOKENS), TOKENS)],
            send_sem=send_sem.at[0, j],
            recv_sem=recv_sem.at[0, here],
            device_id={"tm": base + partner(j)},
        )

    def far(j):
        whole(j, position, partner(j)).start()

    far(across[4])
    far(across[5])

    def kv_copy(chunk, device):
        first, blocks = CHUNKS[chunk]
        return pltpu.make_async_remote_copy(
            src_ref=kv_own.at[:, pl.ds(first, blocks)], dst_ref=kv_prev.at[:, pl.ds(first, blocks)],
            send_sem=kv_send.at[chunk], recv_sem=kv_recv.at[chunk], device_id={"tm": device},
        )

    def kv_twice(chunk):
        first, blocks = CHUNKS[chunk]
        return pltpu.make_async_copy(
            kv_own.at[:, pl.ds(first, blocks)], kv_prev.at[:, pl.ds(first, blocks)], kv_recv.at[chunk]
        )

    def middle_copy(chunk, device):
        return pltpu.make_async_remote_copy(
            src_ref=kv_own.at[:, pl.ds(chunk - 1, 1)], dst_ref=kv_prev.at[:, pl.ds(CHUNKS[chunk][0], 1)],
            send_sem=kv_send.at[chunk], recv_sem=kv_recv.at[chunk], device_id={"tm": device},
        )

    passes = jnp.logical_and(jnp.logical_not(last), position != HALF - 1)
    takes = jnp.logical_and(me > 0, position != HALF)

    def place(first, blocks):
        block = sum(lax.rem(bits[i + 2] + ((first >> i) & 1), 2) * (1 << i) for i in range(2))
        block = block // blocks * blocks
        return pl.ds(pl.multiple_of(block * ROWS_Q, blocks * ROWS_Q), blocks * ROWS_Q)

    wkv_copy.wait()
    wq_copy.wait()

    def keys_values(hidden, target, first, blocks):
        count_rows = blocks * ROWS_Q
        parts = [h.astype(jnp.float32) for h in hidden]
        mean = sum(jnp.sum(p * p, axis=-1, keepdims=True) for p in parts) / width
        inverse = lax.rsqrt(mean + epsilon)
        for stage in range(STAGES):
            normed[:count_rows, stage * PAIR:(stage + 1) * PAIR] = (
                parts[stage] * inverse * gains[STAGES + stage]
            ).astype(jnp.bfloat16)
        pairs = dot(normed[:count_rows], wkv_buf[...])
        for b in range(blocks):
            rows_b = slice(b * ROWS_Q, (b + 1) * ROWS_Q)
            for i in range(KVH):
                target[i, first + b] = pairs[rows_b, i * HD:(i + 1) * HD].astype(jnp.bfloat16)
                values = pairs[rows_b, (KVH + i) * HD:(KVH + i + 1) * HD]
                target[KVH + i, first + b] = values.T.astype(jnp.bfloat16)

    def project(chunk):
        first, blocks = CHUNKS[chunk]
        count_rows = blocks * ROWS_Q
        for j in range(max(4 * first, 1), 4 * (first + blocks)):
            if j in across[4:]:
                whole(j, partner(j), position).wait_recv()
            else:
                for stage in range(STAGES):
                    arrival(stage, j).wait_recv()
        span = place(first, blocks)
        keys_values([recv[stage, span] for stage in range(STAGES)], kv_own, first, blocks)

        @pl.when(passes)
        def _():
            kv_copy(chunk, me + 1).start()

        @pl.when(me == 0)
        def _():
            kv_twice(chunk).start()

        if chunk < 2:
            far(across[6 + chunk])

        for step in range(STAGES):
            q_pair = dot(normed[:count_rows], wq_buf[:, step * PAIR:(step + 1) * PAIR]).astype(jnp.bfloat16)
            for half in range(2):
                queries[2 * step + half, first * ROWS_Q:(first + blocks) * ROWS_Q] = q_pair[:, half * HD:(half + 1) * HD]

    def earlier(chunk):
        @pl.when(me == 0)
        def _():
            kv_twice(chunk).wait()

        @pl.when(takes)
        def _():
            kv_copy(chunk, me - 1).wait_recv()

        if chunk:
            @pl.when(position == HALF)
            def _():
                middle_copy(chunk, me - 1).wait_recv()

    factor = math.log2(math.e) / math.sqrt(HD)
    sharing = HEADS // KVH

    def attend(pieces):
        tasks = [(*p, head) for p in pieces for head in range(HEADS)]

        def scores(task):
            q_first, q_blocks, blocks, _, _, head = task
            keys = jnp.concatenate([ref[head // sharing, b] for ref, b in blocks], axis=0)
            return dot_t(keys, queries[head, q_first * ROWS_Q:(q_first + q_blocks) * ROWS_Q])

        def finish(task, s):
            q_first, q_blocks, blocks, fresh, final, head = task
            columns = slice(q_first * ROWS_Q, (q_first + q_blocks) * ROWS_Q)
            values = jnp.concatenate([ref[KVH + head // sharing, b] for ref, b in blocks], axis=1)
            m = jnp.max(s, axis=0, keepdims=True)
            if not fresh:
                m = jnp.maximum(m, m_run[head, :, columns])
            p = jnp.exp2((s - m) * factor)
            total = jnp.sum(p, axis=0, keepdims=True)
            o = dot(values, p.astype(jnp.bfloat16))
            if not fresh:
                scale = jnp.exp2((m_run[head, :, columns] - m) * factor)
                total = total + l_run[head, :, columns] * scale
                o = o + o_run[head, :, columns] * scale
            if not final:
                m_run[head, :, columns] = m
                l_run[head, :, columns] = total
                o_run[head, :, columns] = o
                return
            out = (o / total).T.astype(jnp.bfloat16)
            done = 0
            for first, chunk_blocks in CHUNKS:
                if q_first <= first < q_first + q_blocks:
                    size = chunk_blocks * ROWS_Q
                    out_s[head, place(first, chunk_blocks)] = out[done:done + size]
                    done += size

        ahead = scores(tasks[0])
        for t, task in enumerate(tasks):
            s = ahead
            if t + 1 < len(tasks):
                ahead = scores(tasks[t + 1])
            finish(task, s)

    own = [(kv_own, b) for b in range(QUARTERS)]
    prev = [(kv_prev, b) for b in range(QUARTERS)]
    with jax.named_scope("proj0"):
        project(0)
    with jax.named_scope("att0"):
        attend([(0, 2, own[:2], True, False)])
    with jax.named_scope("proj1"):
        project(1)

    @pl.when(position == HALF - 1)
    def _():
        for chunk in range(1, len(CHUNKS)):
            middle_copy(chunk, me + 1).start()

    with jax.named_scope("att1"):
        attend([(0, 2, own[2:3], False, False), (2, 1, own[:3], True, False)])

    @pl.when(position == HALF)
    def _():
        for stage in range(STAGES):
            for k in range(1, HALF):
                extra_piece(stage, k).wait_recv()
        keys_values([extra[stage] for stage in range(STAGES)], kv_prev, 0, 2)

    with jax.named_scope("ear0"):
        earlier(0)
    with jax.named_scope("att2"):
        attend([(0, 3, prev[:2], False, False)])

    def third():
        with jax.named_scope("ear1"):
            earlier(1)
        with jax.named_scope("att2b"):
            attend([(0, 3, prev[2:3], False, False)])

    @pl.when(position != HALF)
    def _():
        third()

    with jax.named_scope("proj2"):
        project(2)
    with jax.named_scope("att3"):
        attend([(3, 1, own + prev[:2], True, False)])

    @pl.when(position == HALF)
    def _():
        third()

    with jax.named_scope("ear2"):
        earlier(2)
    with jax.named_scope("att4"):
        attend([(0, 3, own[3:] + prev[3:], False, True), (3, 1, prev[2:], False, True)])

    def sent(stage, _):
        for j in across[:4] + near + beside:
            piece(stage, j).wait_send()
        return 0

    lax.fori_loop(0, STAGES, sent, 0)
    for j in across[4:]:
        whole(j, position, partner(j)).wait_send()

    for chunk in range(len(CHUNKS)):
        @pl.when(passes)
        def _():
            kv_copy(chunk, me + 1).wait_send()

    @pl.when(position == HALF - 1)
    def _():
        for chunk in range(1, len(CHUNKS)):
            middle_copy(chunk, me + 1).wait_send()

    @pl.when(position > HALF)
    def _():
        for stage in range(STAGES):
            extra_piece(stage, lax.rem(position, HALF)).wait_send()


def leave(out_s, out_hbm, out_sem):
    def out_copy(step):
        return pltpu.make_async_copy(out_s.at[step], out_hbm.at[0, :, pl.ds(step * HD, HD)], out_sem.at[step])

    for step in range(HEADS):
        out_copy(step).start()
    for step in range(HEADS):
        out_copy(step).wait()


def body(count, space_time, w_lin, gain_lin, w_query, w_kv, frame_attention_gain):
    rows, width = space_time.shape[1:]
    args = [space_time, w_lin, gain_lin, w_query, w_kv, frame_attention_gain]
    hbm = pl.BlockSpec(memory_space=pltpu.HBM)
    vmem = pl.BlockSpec(memory_space=pltpu.VMEM)
    specs = [hbm, hbm, vmem, hbm, hbm, vmem]
    if count > SB:
        args.append(carried_state(space_time[0], w_lin, count))
        specs.append(vmem)
    bf16, f32 = jnp.bfloat16, jnp.float32
    heads = pl.pallas_call(
        functools.partial(kernel, count),
        out_shape=pltpu.VMEM((HEADS, P_SIZE, HD), bf16),
        in_specs=specs,
        out_specs=vmem,
        scratch_shapes=[
            pltpu.VMEM((rows, width), bf16),
            pltpu.VMEM((STAGES, 3, width, PAIR), bf16),
            pltpu.VMEM(w_query.shape, bf16),
            pltpu.VMEM(w_kv.shape, bf16),
            pltpu.VMEM((2 * STAGES, 1, PAIR), f32),
            pltpu.VMEM((3, rows, PAIR), bf16),
            pltpu.VMEM((STAGES, rows, PAIR), bf16),
            pltpu.VMEM((STAGES, P_SIZE, PAIR), bf16),
            pltpu.VMEM((2 * ROWS_Q, width), bf16),
            pltpu.VMEM((2 * KVH, QUARTERS, ROWS_Q, HD), bf16),
            pltpu.VMEM((2 * KVH, QUARTERS, ROWS_Q, HD), bf16),
            pltpu.VMEM((HEADS, P_SIZE, HD), bf16),
            pltpu.VMEM((HEADS, HD, P_SIZE), f32),
            pltpu.VMEM((HEADS, 1, P_SIZE), f32),
            pltpu.VMEM((HEADS, 1, P_SIZE), f32),
            pltpu.VMEM((STAGES, HALF * TOKENS, PAIR), bf16),
            pltpu.SemaphoreType.DMA((3,)),
            pltpu.SemaphoreType.DMA((STAGES, 3)),
            pltpu.SemaphoreType.DMA((STAGES, SB)),
            pltpu.SemaphoreType.DMA((STAGES, SB)),
            pltpu.SemaphoreType.DMA((len(CHUNKS),)),
            pltpu.SemaphoreType.DMA((len(CHUNKS),)),
            pltpu.SemaphoreType.DMA((STAGES,)),
            pltpu.SemaphoreType.DMA((STAGES, HALF)),
        ],
        compiler_params=pltpu.CompilerParams(
            collective_id=0, has_side_effects=True, vmem_limit_bytes=60 * 1024 * 1024
        ),
        name="video_layer",
    )(*args)
    return pl.pallas_call(
        leave,
        out_shape=jax.ShapeDtypeStruct(space_time.shape, bf16),
        in_specs=[vmem],
        out_specs=hbm,
        scratch_shapes=[pltpu.SemaphoreType.DMA((HEADS,))],
        compiler_params=pltpu.CompilerParams(vmem_limit_bytes=4 * 1024 * 1024),
        name="leave",
    )(heads)


def solution(mesh):
    placed = (P(("groups", "tm"), None, None), P(), P(), P(), P(), P())
    return jax.shard_map(
        functools.partial(body, mesh.shape["tm"]),
        mesh=mesh,
        in_specs=placed,
        out_specs=P(("groups", "tm"), None, None),
        check_vma=False,
    )
```

```python
import functools
import math

import jax
import jax.numpy as jnp
from jax import lax
from jax.experimental import pallas as pl
from jax.experimental.pallas import tpu as pltpu
from jax.sharding import PartitionSpec as P

HEADS = 8
HD = 128
KVH = 2
P_SIZE = 512
SB = 16
SPAN = 128
PAIR = 2 * HD
STAGES = HEADS // 2
TOKENS = P_SIZE // SB
QUARTERS = 4
ROWS_Q = P_SIZE // QUARTERS
HALF = SB // 2
CHUNKS = [(0, 2), (2, 1), (3, 1)]

epsilon = 1e-06


def shifted(block, axis, distance):
    devices = range(lax.axis_size(axis))
    route = [(i - distance, i) for i in devices if i - distance in devices]
    return lax.ppermute(block, axis, route)


def carried_state(tokens, w_lin, count):
    width = tokens.shape[1]
    rows = tokens.shape[0]
    packed = jnp.dot(tokens, w_lin[:, width:], preferred_element_type=jnp.float32).astype(jnp.bfloat16)
    keys = packed[:, :width].reshape(rows, HEADS, HD)
    values = packed[:, width:].reshape(rows, HEADS, HD)
    total = jnp.einsum("nhd,nhe->hde", keys, values, preferred_element_type=jnp.float32)
    within = lax.axis_index("tm") // SB

    def hop(_, state):
        return jnp.where(within > 0, shifted(state + total, "tm", SB), 0.0)

    return lax.fori_loop(0, count // SB - 1, hop, jnp.zeros_like(total))


def dot(a, b):
    return jnp.dot(a, b, preferred_element_type=jnp.float32)


def dot_t(a, b):
    return lax.dot_general(a, b, (((1,), (1,)), ((), ())), preferred_element_type=jnp.float32)


def t_dot(a, b):
    return lax.dot_general(a, b, (((0,), (0,)), ((), ())), preferred_element_type=jnp.float32)


def kernel(count, *refs):
    long = count > SB
    tokens_hbm, w_lin_hbm, gain_lin, w_query_hbm, w_kv_hbm, gain_frame = refs[:6]
    refs = refs[6:]
    if long:
        incoming = refs[0]
        refs = refs[1:]
    (out_s, tokens, w_buf, wq_buf, wkv_buf, gains, qkv, hid, recv, normed, kv_own, kv_prev, queries, o_run, m_run,
     l_run, extra, in_sem, w_sem, send_sem, recv_sem, kv_send, kv_recv, extra_send, extra_recv) = refs
    width = tokens.shape[1]
    rows = tokens.shape[0]

    me = lax.axis_index("tm")
    position = lax.rem(me, SB)
    base = me - position
    bits = [lax.rem(position // (1 << i), 2) for i in range(4)]

    def partner(j):
        return sum(lax.rem(bits[i] + ((j >> i) & 1), 2) * (1 << i) for i in range(4))

    last = me == count - 1
    barrier = pltpu.get_barrier_semaphore()

    token_copy = pltpu.make_async_copy(tokens_hbm.at[0], tokens, in_sem.at[0])
    token_copy.start()

    def w_copy(stage, c):
        start = c * width + stage * PAIR
        if not isinstance(stage, int):
            start = pl.multiple_of(start, PAIR)
        return pltpu.make_async_copy(
            w_lin_hbm.at[:, pl.ds(start, PAIR)], w_buf.at[stage, c], w_sem.at[stage]
        )

    for c in range(3):
        w_copy(0, c).start()
    wkv_copy = pltpu.make_async_copy(w_kv_hbm, wkv_buf, in_sem.at[1])
    wq_copy = pltpu.make_async_copy(w_query_hbm, wq_buf, in_sem.at[2])

    beside, near, across = [1, 2, 3], [4, 5, 6, 7], list(range(8, SB))
    peers = across + near + beside
    crossing, straight = [10, 11, 14, 15], [8, 9, 12, 13]
    for j in peers:
        pl.semaphore_signal(barrier, inc=1, device_id={"tm": base + partner(j)})
    if long:
        @pl.when(jnp.logical_and(position == SB - 1, jnp.logical_not(last)))
        def _():
            pl.semaphore_signal(barrier, inc=1, device_id={"tm": me + 1})

        @pl.when(jnp.logical_and(position == 0, me > 0))
        def _():
            pl.semaphore_signal(barrier, inc=1, device_id={"tm": me - 1})

    line = gain_lin[...].astype(jnp.float32).reshape(1, width)
    frame = gain_frame[...].astype(jnp.float32).reshape(1, width)
    for stage in range(STAGES):
        gains[stage] = line[:, stage * PAIR:(stage + 1) * PAIR]
        gains[STAGES + stage] = frame[:, stage * PAIR:(stage + 1) * PAIR]

    causal = lax.broadcasted_iota(jnp.int32, (SPAN, SPAN), 0) >= lax.broadcasted_iota(jnp.int32, (SPAN, SPAN), 1)

    def piece(stage, j):
        other = partner(j)
        return pltpu.make_async_remote_copy(
            src_ref=hid.at[stage, pl.ds(pl.multiple_of(other * TOKENS, TOKENS), TOKENS)],
            dst_ref=recv.at[stage, pl.ds(pl.multiple_of(position * TOKENS, TOKENS), TOKENS)],
            send_sem=send_sem.at[0],
            recv_sem=recv_sem.at[1 if j in crossing else 0],
            device_id={"tm": base + other},
        )

    def all_of(chunk):
        first, blocks = CHUNKS[chunk]
        tokens_in = 4 * blocks * TOKENS - (TOKENS if chunk == 0 else 0)
        return pltpu.make_async_remote_copy(
            src_ref=hid.at[:, :tokens_in], dst_ref=recv.at[:, :tokens_in], send_sem=send_sem.at[0],
            recv_sem=recv_sem.at[chunk], device_id={"tm": base + partner(1)},
        )

    def all_sent():
        tokens_out = (SB - 1) * TOKENS
        return pltpu.make_async_remote_copy(
            src_ref=hid.at[:, :tokens_out], dst_ref=recv.at[:, :tokens_out], send_sem=send_sem.at[0],
            recv_sem=recv_sem.at[0], device_id={"tm": base + partner(1)},
        )

    def all_extra():
        tokens_in = (HALF - 1) * TOKENS
        return pltpu.make_async_remote_copy(
            src_ref=extra.at[:, :tokens_in], dst_ref=extra.at[:, :tokens_in], send_sem=extra_send.at[0],
            recv_sem=extra_recv.at[0], device_id={"tm": base + partner(1)},
        )

    def extra_sent():
        return pltpu.make_async_remote_copy(
            src_ref=hid.at[:, :TOKENS], dst_ref=recv.at[:, :TOKENS], send_sem=extra_send.at[0],
            recv_sem=extra_recv.at[0], device_id={"tm": base + partner(1)},
        )

    def extra_piece(stage, k):
        return pltpu.make_async_remote_copy(
            src_ref=hid.at[stage, pl.ds((HALF - 1) * TOKENS, TOKENS)],
            dst_ref=extra.at[stage, pl.ds(pl.multiple_of(k * TOKENS, TOKENS), TOKENS)],
            send_sem=extra_send.at[0],
            recv_sem=extra_recv.at[0],
            device_id={"tm": base + HALF},
        )

    token_copy.wait()

    def mix(stage, _):
        pltpu.make_async_copy(w_buf.at[stage], w_buf.at[stage], w_sem.at[stage]).wait()

        @pl.when(stage + 1 < STAGES)
        def _():
            for c in range(3):
                w_copy(stage + 1, c).start()

        @pl.when(stage + 1 == STAGES)
        def _():
            wkv_copy.start()
            wq_copy.start()

        for c in range(3):
            qkv[c] = dot(tokens[...], w_buf[stage, c]).astype(jnp.bfloat16)
        states = [incoming[2 * stage + half] if long else jnp.zeros((HD, HD), jnp.float32) for half in range(2)]

        def spans(numbers):
            for b, half in [(b, half) for b in numbers for half in range(2)]:
                columns = slice(half * HD, (half + 1) * HD)
                state = states[half]
                gain = gains[stage][:, columns]
                wide = pl.ds(pl.multiple_of(stage * PAIR + half * HD, HD), HD)
                span = slice(b * SPAN, (b + 1) * SPAN)
                q, k, v = qkv[0, span, columns], qkv[1, span, columns], qkv[2, span, columns]
                local = jnp.where(causal, dot_t(q, k), 0.0).astype(jnp.bfloat16)
                if b == 0 and not long:
                    mixed = dot(local, v)
                else:
                    mixed = dot(
                        jnp.concatenate([q, local], axis=1),
                        jnp.concatenate([state.astype(jnp.bfloat16), v], axis=0),
                    )
                if b + 1 < rows // SPAN:
                    states[half] = state + t_dot(k, v)
                mean = jnp.mean(mixed * mixed, axis=-1, keepdims=True)
                grown = mixed * lax.rsqrt(mean + epsilon) * gain
                hid[stage, span, columns] = (tokens[span, wide].astype(jnp.float32) + grown).astype(jnp.bfloat16)

        def send(group):
            for j in group:
                piece(stage, j).start()

        middle = rows // SPAN // 2
        spans(range(middle))

        @pl.when(stage == 0)
        def _():
            extra = 0
            if long:
                extra = (
                    jnp.logical_and(position == SB - 1, jnp.logical_not(last)).astype(jnp.int32)
                    + jnp.logical_and(position == 0, me > 0).astype(jnp.int32)
                )
            pl.semaphore_wait(barrier, SB - 1 + extra)

        @pl.when(jnp.logical_and(bits[3] == 1, stage < STAGES - 1))
        def _():
            send(crossing)

        @pl.when(position > HALF)
        def _():
            extra_piece(stage, lax.rem(position, HALF)).start()

        @pl.when(position == HALF)
        def _():
            extra[stage, :TOKENS] = hid[stage, (HALF - 1) * TOKENS:HALF * TOKENS]

        @pl.when(bits[3] == 0)
        def _():
            send(near + beside)

        spans(range(middle, rows // SPAN))

        @pl.when(bits[3] == 1)
        def _():
            send(near + beside)

        @pl.when(jnp.logical_or(bits[3] == 0, stage == STAGES - 1))
        def _():
            send(crossing)

        mine = pl.ds(pl.multiple_of(position * TOKENS, TOKENS), TOKENS)
        recv[stage, mine] = hid[stage, mine]
        return 0

    lax.fori_loop(0, STAGES, mix, 0)

    def whole(j, here, there):
        return pltpu.make_async_remote_copy(
            src_ref=hid.at[:, pl.ds(pl.multiple_of(there * TOKENS, TOKENS), TOKENS)],
            dst_ref=recv.at[:, pl.ds(pl.multiple_of(here * TOKENS, TOKENS), TOKENS)],
            send_sem=send_sem.at[0],
            recv_sem=recv_sem.at[2],
            device_id={"tm": base + partner(j)},
        )

    def far(j):
        whole(j, position, partner(j)).start()

    for j in straight:
        far(j)

    def kv_copy(chunk, device):
        first, blocks = CHUNKS[chunk]
        return pltpu.make_async_remote_copy(
            src_ref=kv_own.at[:, pl.ds(first, blocks)], dst_ref=kv_prev.at[:, pl.ds(first, blocks)],
            send_sem=kv_send.at[chunk], recv_sem=kv_recv.at[chunk], device_id={"tm": device},
        )

    def kv_twice(chunk):
        first, blocks = CHUNKS[chunk]
        return pltpu.make_async_copy(
            kv_own.at[:, pl.ds(first, blocks)], kv_prev.at[:, pl.ds(first, blocks)], kv_recv.at[chunk]
        )

    def middle_copy(chunk, device):
        return pltpu.make_async_remote_copy(
            src_ref=kv_own.at[:, pl.ds(chunk - 1, 1)], dst_ref=kv_prev.at[:, pl.ds(CHUNKS[chunk][0], 1)],
            send_sem=kv_send.at[chunk], recv_sem=kv_recv.at[chunk], device_id={"tm": device},
        )

    passes = jnp.logical_and(jnp.logical_not(last), position != HALF - 1)
    takes = jnp.logical_and(me > 0, position != HALF)

    def place(first, blocks):
        if blocks == 2:
            return [pl.ds(pl.multiple_of(2 * bits[3] * ROWS_Q, 2 * ROWS_Q), 2 * ROWS_Q)]
        row = 1 - bits[1] if first == 2 else bits[1]
        size = ROWS_Q // 2
        return [
            pl.ds(pl.multiple_of((2 * (1 - bits[3]) + plane) * ROWS_Q + row * size, size), size) for plane in range(2)
        ]

    wkv_copy.wait()
    wq_copy.wait()

    def keys_values(hidden, target, first, blocks):
        count_rows = blocks * ROWS_Q
        parts = [h.astype(jnp.float32) for h in hidden]
        mean = sum(jnp.sum(p * p, axis=-1, keepdims=True) for p in parts) / width
        inverse = lax.rsqrt(mean + epsilon)
        for stage in range(STAGES):
            normed[:count_rows, stage * PAIR:(stage + 1) * PAIR] = (
                parts[stage] * inverse * gains[STAGES + stage]
            ).astype(jnp.bfloat16)
        pairs = dot(normed[:count_rows], wkv_buf[...])
        for b in range(blocks):
            rows_b = slice(b * ROWS_Q, (b + 1) * ROWS_Q)
            for i in range(KVH):
                target[i, first + b] = pairs[rows_b, i * HD:(i + 1) * HD].astype(jnp.bfloat16)
                values = pairs[rows_b, (KVH + i) * HD:(KVH + i + 1) * HD]
                target[KVH + i, first + b] = values.T.astype(jnp.bfloat16)

    def project(chunk):
        first, blocks = CHUNKS[chunk]
        count_rows = blocks * ROWS_Q
        all_of(chunk).wait_recv()
        spans = place(first, blocks)
        parts = [jnp.concatenate([recv[stage, span] for span in spans], axis=0) for stage in range(STAGES)]
        keys_values(parts, kv_own, first, blocks)

        @pl.when(passes)
        def _():
            kv_copy(chunk, me + 1).start()

        @pl.when(me == 0)
        def _():
            kv_twice(chunk).start()

        for step in range(STAGES):
            q_pair = dot(normed[:count_rows], wq_buf[:, step * PAIR:(step + 1) * PAIR]).astype(jnp.bfloat16)
            for half in range(2):
                queries[2 * step + half, first * ROWS_Q:(first + blocks) * ROWS_Q] = q_pair[:, half * HD:(half + 1) * HD]

    def earlier(chunk):
        @pl.when(me == 0)
        def _():
            kv_twice(chunk).wait()

        @pl.when(takes)
        def _():
            kv_copy(chunk, me - 1).wait_recv()

        if chunk:
            @pl.when(position == HALF)
            def _():
                middle_copy(chunk, me - 1).wait_recv()

    factor = math.log2(math.e) / math.sqrt(HD)
    sharing = HEADS // KVH

    def attend(pieces):
        tasks = [(*p, head) for p in pieces for head in range(HEADS)]

        def scores(task):
            q_first, q_blocks, blocks, _, _, head = task
            keys = jnp.concatenate([ref[head // sharing, b] for ref, b in blocks], axis=0)
            return dot_t(keys, queries[head, q_first * ROWS_Q:(q_first + q_blocks) * ROWS_Q])

        def finish(task, s):
            q_first, q_blocks, blocks, fresh, final, head = task
            columns = slice(q_first * ROWS_Q, (q_first + q_blocks) * ROWS_Q)
            values = jnp.concatenate([ref[KVH + head // sharing, b] for ref, b in blocks], axis=1)
            m = jnp.max(s, axis=0, keepdims=True)
            if not fresh:
                m = jnp.maximum(m, m_run[head, :, columns])
            p = jnp.exp2((s - m) * factor)
            total = jnp.sum(p, axis=0, keepdims=True)
            o = dot(values, p.astype(jnp.bfloat16))
            if not fresh:
                scale = jnp.exp2((m_run[head, :, columns] - m) * factor)
                total = total + l_run[head, :, columns] * scale
                o = o + o_run[head, :, columns] * scale
            if not final:
                m_run[head, :, columns] = m
                l_run[head, :, columns] = total
                o_run[head, :, columns] = o
                return
            out = (o / total).T.astype(jnp.bfloat16)
            done = 0
            for first, chunk_blocks in CHUNKS:
                if q_first <= first < q_first + q_blocks:
                    for span in place(first, chunk_blocks):
                        out_s[head, span] = out[done:done + span.size]
                        done += span.size

        ahead = scores(tasks[0])
        for t, task in enumerate(tasks):
            s = ahead
            if t + 1 < len(tasks):
                ahead = scores(tasks[t + 1])
            finish(task, s)

    own = [(kv_own, b) for b in range(QUARTERS)]
    prev = [(kv_prev, b) for b in range(QUARTERS)]
    with jax.named_scope("proj0"):
        project(0)
    with jax.named_scope("att0"):
        attend([(0, 2, own[:2], True, False)])
    with jax.named_scope("proj1"):
        project(1)

    @pl.when(position == HALF - 1)
    def _():
        for chunk in range(1, len(CHUNKS)):
            middle_copy(chunk, me + 1).start()

    with jax.named_scope("att1"):
        attend([(0, 2, own[2:3], False, False), (2, 1, own[:3], True, False)])

    @pl.when(position == HALF)
    def _():
        all_extra().wait_recv()
        keys_values([extra[stage] for stage in range(STAGES)], kv_prev, 0, 2)

    with jax.named_scope("ear0"):
        earlier(0)
    with jax.named_scope("att2"):
        attend([(0, 3, prev[:2], False, False)])

    def third():
        with jax.named_scope("ear1"):
            earlier(1)
        with jax.named_scope("att2b"):
            attend([(0, 3, prev[2:3], False, False)])

    @pl.when(position != HALF)
    def _():
        third()

    with jax.named_scope("proj2"):
        project(2)
    with jax.named_scope("att3"):
        attend([(3, 1, own + prev[:2], True, False)])

    @pl.when(position == HALF)
    def _():
        third()

    with jax.named_scope("ear2"):
        earlier(2)
    with jax.named_scope("att4"):
        attend([(0, 3, own[3:] + prev[3:], False, True), (3, 1, prev[2:], False, True)])

    all_sent().wait_send()

    for chunk in range(len(CHUNKS)):
        @pl.when(passes)
        def _():
            kv_copy(chunk, me + 1).wait_send()

    @pl.when(position == HALF - 1)
    def _():
        for chunk in range(1, len(CHUNKS)):
            middle_copy(chunk, me + 1).wait_send()

    @pl.when(position > HALF)
    def _():
        extra_sent().wait_send()


def leave(out_s, out_hbm, out_sem):
    def out_copy(step):
        return pltpu.make_async_copy(out_s.at[step], out_hbm.at[0, :, pl.ds(step * HD, HD)], out_sem.at[step])

    for step in range(HEADS):
        out_copy(step).start()
    for step in range(HEADS):
        out_copy(step).wait()


def body(count, space_time, w_lin, gain_lin, w_query, w_kv, frame_attention_gain):
    rows, width = space_time.shape[1:]
    args = [space_time, w_lin, gain_lin, w_query, w_kv, frame_attention_gain]
    hbm = pl.BlockSpec(memory_space=pltpu.HBM)
    vmem = pl.BlockSpec(memory_space=pltpu.VMEM)
    specs = [hbm, hbm, vmem, hbm, hbm, vmem]
    if count > SB:
        args.append(carried_state(space_time[0], w_lin, count))
        specs.append(vmem)
    bf16, f32 = jnp.bfloat16, jnp.float32
    heads = pl.pallas_call(
        functools.partial(kernel, count),
        out_shape=pltpu.VMEM((HEADS, P_SIZE, HD), bf16),
        in_specs=specs,
        out_specs=vmem,
        scratch_shapes=[
            pltpu.VMEM((rows, width), bf16),
            pltpu.VMEM((STAGES, 3, width, PAIR), bf16),
            pltpu.VMEM(w_query.shape, bf16),
            pltpu.VMEM(w_kv.shape, bf16),
            pltpu.VMEM((2 * STAGES, 1, PAIR), f32),
            pltpu.VMEM((3, rows, PAIR), bf16),
            pltpu.VMEM((STAGES, rows, PAIR), bf16),
            pltpu.VMEM((STAGES, P_SIZE, PAIR), bf16),
            pltpu.VMEM((2 * ROWS_Q, width), bf16),
            pltpu.VMEM((2 * KVH, QUARTERS, ROWS_Q, HD), bf16),
            pltpu.VMEM((2 * KVH, QUARTERS, ROWS_Q, HD), bf16),
            pltpu.VMEM((HEADS, P_SIZE, HD), bf16),
            pltpu.VMEM((HEADS, HD, P_SIZE), f32),
            pltpu.VMEM((HEADS, 1, P_SIZE), f32),
            pltpu.VMEM((HEADS, 1, P_SIZE), f32),
            pltpu.VMEM((STAGES, HALF * TOKENS, PAIR), bf16),
            pltpu.SemaphoreType.DMA((3,)),
            pltpu.SemaphoreType.DMA((STAGES,)),
            pltpu.SemaphoreType.DMA((1,)),
            pltpu.SemaphoreType.DMA((len(CHUNKS),)),
            pltpu.SemaphoreType.DMA((len(CHUNKS),)),
            pltpu.SemaphoreType.DMA((len(CHUNKS),)),
            pltpu.SemaphoreType.DMA((1,)),
            pltpu.SemaphoreType.DMA((1,)),
        ],
        compiler_params=pltpu.CompilerParams(
            collective_id=0, has_side_effects=True, vmem_limit_bytes=60 * 1024 * 1024
        ),
        name="video_layer",
    )(*args)
    return pl.pallas_call(
        leave,
        out_shape=jax.ShapeDtypeStruct(space_time.shape, bf16),
        in_specs=[vmem],
        out_specs=hbm,
        scratch_shapes=[pltpu.SemaphoreType.DMA((HEADS,))],
        compiler_params=pltpu.CompilerParams(vmem_limit_bytes=4 * 1024 * 1024),
        name="leave",
    )(heads)


def solution(mesh):
    placed = (P(("groups", "tm"), None, None), P(), P(), P(), P(), P())
    return jax.shard_map(
        functools.partial(body, mesh.shape["tm"]),
        mesh=mesh,
        in_specs=placed,
        out_specs=P(("groups", "tm"), None, None),
        check_vma=False,
    )
```
